128 devices in a mesh: hi: 8 (over z, x_lo), lo: 16 (over x_hi, y, core).
Axes of the slice: x: 4 (x_hi: 2, x_lo: 2; x = x_hi * 2 + x_lo), y: 4, z: 4, core: 2. Of those that a mesh axis runs over, the one named last changes fastest.
Arguments:
- stem: float32 [1024, 256, 1024], P(('hi', 'lo')), may hold values from -6 to 6
- first_branch: float32 [8, 1024, 1024], P(None, 'lo'), may hold values from -0.1875 to 0.1875
- second_branch: float32 [8, 1024, 1024], P(None, 'lo'), may hold values from -0.1875 to 0.1875
- assign: int32 [2], replicated, may hold values from 0 to 7
Outputs:
- contracted: float32 [1024, 256, 1024], P(('hi', 'lo'))
The draws below stay inside these ranges and needn't reach their ends.
Inputs may be any that keep to these rules, and one draw needn't show every extreme that they name: assign[0] selects the first branch's slice, assign[1] the second's.
All inputs are finite; a program needn't handle non-finite values.
Results may differ from the reference program's by a relative error of at most 0.00007.
Values sent between devices are 32-bit elements; how exact they have to be, the bound alone decides.
A program may use at most 128 MiB of HBM per device.

```python
import jax
import jax.numpy as jnp
from jax import lax

WJ = 1024
MID = 256
WI = 1024
SLICES = 8


def level_of(own_key, shape, cuts, smallest, high):
    factor_of = 1.0
    for dim, shards_of in cuts:
        heights = jax.random.uniform(jax.random.fold_in(jax.random.fold_in(own_key, 6), dim), (shards_of,), jnp.float32, smallest / len(cuts), high / len(cuts))
        factor_of = factor_of * jnp.repeat(jnp.exp(heights), shape[dim] // shards_of).reshape((-1,) + (1,) * (len(shape) - 1 - dim))
    return factor_of


def gaussian(stream_key, dims, deviation, limit, split=(), dtype=jnp.bfloat16):
    entries = deviation * jax.random.normal(stream_key, dims, jnp.float32)
    if split:
        entries = entries * level_of(stream_key, dims, split, -0.22, 0.18)
    return jnp.clip(entries, -limit, limit).astype(dtype)


def setup_inputs(seed: int = 0) -> dict:
    keys = jax.random.split(jax.random.key(seed), 5)
    return {
        "stem": gaussian(keys[0], (WJ, MID, WI), 1.0, 6.0, ((0, 128),), jnp.float32),
        "first_branch": gaussian(keys[1], (SLICES, WI, WI), WI ** -0.5, 0.1875, ((1, 16),), jnp.float32),
        "second_branch": gaussian(keys[2], (SLICES, WJ, WJ), WJ ** -0.5, 0.1875, ((1, 16),), jnp.float32),
        "assign": jax.random.randint(keys[3], (2,), 0, SLICES).astype(jnp.int32),
    }


def reference(stem, first_branch, second_branch, assign):
    first = lax.dynamic_index_in_dim(first_branch, assign[0], 0, keepdims=False)
    second = lax.dynamic_index_in_dim(second_branch, assign[1], 0, keepdims=False)
    wide_j, middle, wide_i = stem.shape
    absorbed = jnp.dot(stem.reshape(wide_j * middle, wide_i), first, precision=lax.Precision.HIGHEST, preferred_element_type=jnp.float32)
    absorbed = absorbed.reshape(wide_j, middle * wide_i)
    contracted = lax.dot_general(second, absorbed, (((0,), (0,)), ((), ())), precision=lax.Precision.HIGHEST, preferred_element_type=jnp.float32)
    return contracted.reshape(wide_j, middle, wide_i)
```

```python
import functools

import jax
import jax.numpy as jnp
from jax import lax
from jax.experimental import pallas as pl
from jax.experimental.pallas import tpu as pltpu
from jax.sharding import PartitionSpec as P

MESH = pl.DeviceIdType.MESH
F32, BF16 = jnp.float32, jnp.bfloat16
N = 128
W = 1024
R = W // N
CH = 32
A = 32
Q = 8


def split(v):
    top = v.astype(BF16)
    return top, (v - top.astype(F32)).astype(BF16)


def dot3(ah, al, bh, bl):
    d = functools.partial(jnp.dot, preferred_element_type=F32)
    return d(ah, bh) + (d(ah, bl) + d(al, bh))


def device_at(x, y, z, c):
    return z * 2 + x % 2, (x // 2) * 8 + y * 2 + c


def kernel(stem, f_piece, s_piece, home, stage, turned, spread, f_all, s_all, fh, fl, sh, sl, yh, yl,
           stage_sem, own_sem, self_sem, g_send, g_recv, x_send, x_recv, z_send, z_recv):
    hi, lo = lax.axis_index("hi"), lax.axis_index("lo")
    me = hi * 16 + lo
    x, y, z, c = (lo // 8) * 2 + hi % 2, (lo // 2) % 4, hi // 2, lo % 2
    chip = lo // 2

    def load(q, slot):
        pltpu.make_async_copy(stem.at[:, pl.ds(q * CH, CH)], stage.at[slot], stage_sem.at[slot]).start()

    def relay(q, slot):
        pltpu.make_async_copy(stage.at[slot], stage.at[slot], stage_sem.at[slot]).wait()

        def one(t, _):
            block = stage[slot, :, pl.ds(pl.multiple_of(t * 8, 8), 8), :]
            rows = pl.ds(pl.multiple_of((q * CH + t * 8) * R, 8 * R), 8 * R)
            turned[rows, :] = pltpu.einshape("jmi->mji", block).reshape(8 * R, W)
            return 0

        lax.fori_loop(0, CH // 8, one, 0)

    own_f = pltpu.make_async_copy(f_piece, f_all.at[chip, c], own_sem.at[0])
    own_s = pltpu.make_async_copy(s_piece, s_all.at[chip, c], own_sem.at[1])
    own_f.start()
    own_s.start()
    for q in range(4):
        load(q, q)

    own_f.wait()
    own_s.wait()
    barrier = pltpu.get_barrier_semaphore()

    def greet(t, _):
        p = (me + t) % N
        pl.semaphore_signal(barrier, inc=1, device_id=(p // 16, p % 16), device_id_type=MESH)
        return 0

    lax.fori_loop(1, N, greet, 0)
    for q in range(4):
        relay(q, q)
        load(q + 4, q)
    pl.semaphore_wait(barrier, N - 1)

    def remote(src, dst, send, recv, target):
        return pltpu.make_async_remote_copy(
            src_ref=src, dst_ref=dst, send_sem=send, recv_sem=recv, device_id=target, device_id_type=MESH
        )

    def group(t, _):
        gx, gy = (x + 2 * (t // 4)) % 4, (y + t % 4) % 4
        target = device_at(gx, gy, z, c)
        for n, ref in enumerate((f_all, s_all)):
            for rows in (pl.ds(0, A), pl.ds(pl.multiple_of(A + z * Q, Q), Q)):
                part = ref.at[chip, c, rows]
                remote(part, part, g_send.at[n, 0], g_recv.at[n, 0], target).start()
        return 0

    lax.fori_loop(1, 8, group, 0)

    def offset(t):
        dc, u = t // 64, t % 64
        a, b, g = u % 4, (u // 4) % 4, u // 16
        target = device_at((x + a) % 4, (y + a + b) % 4, (z + a + b + g) % 4, (c + dc) % 2)
        return target, target[0] * 16 + target[1]

    my_rows = pl.ds(pl.multiple_of(me * R, R), R)

    def send_out(h):
        def one(t, _):
            target, p = offset(t)
            src = turned.at[pl.ds(pl.multiple_of((h * N + p) * R, R), R)]
            remote(src, spread.at[h, my_rows], x_send.at[h], x_recv.at[h], target).start()
            return 0

        lax.fori_loop(1, N, one, 0)
        own = pl.ds(pl.multiple_of((h * N + me) * R, R), R)
        pltpu.make_async_copy(turned.at[own], spread.at[h, my_rows], self_sem.at[h]).start()

    def send_home(h):
        own = pl.ds(pl.multiple_of((h * N + me) * R, R), R)

        def one(t, _):
            target, p = offset(t)
            src = spread.at[h, pl.ds(pl.multiple_of(p * R, R), R)]
            remote(src, home.at[own], z_send.at[h], z_recv.at[h], target).start()
            return 0

        lax.fori_loop(1, N, one, 0)
        pltpu.make_async_copy(spread.at[h, my_rows], home.at[own], self_sem.at[2 + h]).start()

    def rows_of(count):
        return spread.at[0, pl.ds(0, count)]

    def drain(count, send=None, recv=None):
        if send is not None:
            remote(rows_of(count), rows_of(count), send, send, (hi, lo)).wait_send()
        if recv is not None:
            remote(rows_of(count), rows_of(count), recv, recv, (hi, lo)).wait_recv()

    send_out(0)
    for q in range(4, 8):
        relay(q, q - 4)

    for n, ref in enumerate((f_all, s_all)):
        drain(7 * (A + Q), recv=g_recv.at[n, 0])
        for t in range(1, 4):
            part = ref.at[:, c, pl.ds(pl.multiple_of(A + z * Q, Q), Q)]
            remote(part, part, g_send.at[n, 1], g_recv.at[n, 1], device_at(x, y, (z + t) % 4, c)).start()
    send_out(1)
    for n, ref in enumerate((f_all, s_all)):
        drain(3 * 8 * Q, recv=g_recv.at[n, 1])
        part = ref.at[:, c]
        remote(part, part, g_send.at[n, 2], g_recv.at[n, 2], device_at(x, y, z, 1 - c)).start()

    drain(512, recv=g_recv.at[0, 2])

    def prepare_f(t, _):
        rows = pl.ds(pl.multiple_of(t * 64, 64), 64)
        fh[rows, :], fl[rows, :] = split(f_all[t // 2, t % 2])
        return 0

    lax.fori_loop(0, 16, prepare_f, 0)
    drain(512, recv=g_recv.at[1, 2])

    def prepare_s(t, _):
        p, cols = t // 8, pl.ds(pl.multiple_of((t % 8) * 128, 128), 128)
        block = jnp.concatenate([s_all[p, 0, :, cols], s_all[p, 1, :, cols]], axis=0)
        to = pl.ds(pl.multiple_of(p * 128, 128), 128)
        sh[cols, to], sl[cols, to] = split(block.T)
        return 0

    lax.fori_loop(0, 64, prepare_s, 0)

    for h in range(2):
        pltpu.make_async_copy(turned.at[pl.ds(0, R)], spread.at[h, my_rows], self_sem.at[h]).wait()
        drain((N - 1) * R, recv=x_recv.at[h])

        def by_first(t, _):
            rows = pl.ds(pl.multiple_of(t * 256, 256), 256)
            ah, al = split(spread[h, rows, :])

            def tile(n, _):
                cols = pl.ds(pl.multiple_of(n * 256, 256), 256)
                yh[rows, cols], yl[rows, cols] = split(dot3(ah, al, fh[:, cols], fl[:, cols]))
                return 0

            return lax.fori_loop(0, 4, tile, 0)

        lax.fori_loop(0, 4, by_first, 0)

        def by_second(t, _):
            rows = pl.ds(pl.multiple_of((t // 4) * 256, 256), 256)
            cols = pl.ds(pl.multiple_of((t % 4) * 256, 256), 256)
            spread[h, rows, cols] = dot3(sh[rows, :], sl[rows, :], yh[:, cols], yl[:, cols])
            return 0

        lax.fori_loop(0, 16, by_second, 0)
        send_home(h)

    for n in range(2):
        drain(7 * (A + Q), send=g_send.at[n, 0])
        drain(3 * 8 * Q, send=g_send.at[n, 1])
        drain(512, send=g_send.at[n, 2])
    for h in range(2):
        drain((N - 1) * R, send=x_send.at[h])
        drain((N - 1) * R, send=z_send.at[h])
        drain((N - 1) * R, recv=z_recv.at[h])
        pltpu.make_async_copy(turned.at[pl.ds(0, R)], spread.at[h, my_rows], self_sem.at[2 + h]).wait()


def exchange(stem, f_piece, s_piece):
    dma = pltpu.SemaphoreType.DMA
    return pl.pallas_call(
        kernel,
        name="exchange",
        out_shape=jax.ShapeDtypeStruct((stem.shape[1] * R, W), F32),
        in_specs=[pl.BlockSpec(memory_space=pl.ANY)] * 3,
        out_specs=pl.BlockSpec(memory_space=pl.ANY),
        scratch_shapes=[
            pltpu.VMEM((4, R, CH, W), F32),
            pltpu.VMEM((2 * W, W), F32),
            pltpu.VMEM((2, W, W), F32),
            pltpu.VMEM((8, 2, 64, W), F32),
            pltpu.VMEM((8, 2, 64, W), F32),
        ]
        + [pltpu.VMEM((W, W), BF16)] * 6
        + [dma((4,)), dma((2,)), dma((4,)), dma((2, 3)), dma((2, 3)), dma((2,)), dma((2,)), dma((2,)), dma((2,))],
        compiler_params=pltpu.CompilerParams(
            collective_id=0, has_side_effects=True, vmem_limit_bytes=60 << 20
        ),
    )(stem, f_piece, s_piece)


def settle_kernel(z_ref, o_ref):
    for t in range(CH // 8):
        block = z_ref[pl.ds(t * 8 * R, 8 * R), :].reshape(8, R, W)
        o_ref[:, pl.ds(t * 8, 8), :] = pltpu.einshape("mlk->lmk", block)


def settle(home):
    m = home.shape[0] // R
    return pl.pallas_call(
        settle_kernel,
        name="settle",
        grid=(m // CH,),
        out_shape=jax.ShapeDtypeStruct((R, m, W), F32),
        in_specs=[pl.BlockSpec((CH * R, W), lambda q: (q, 0))],
        out_specs=pl.BlockSpec((R, CH, W), lambda q: (0, q, 0)),
    )(home)


def body(stem, first_branch, second_branch, assign):
    f_piece = lax.dynamic_index_in_dim(first_branch, assign[0], 0, keepdims=False)
    s_piece = lax.dynamic_index_in_dim(second_branch, assign[1], 0, keepdims=False)
    return settle(exchange(stem, f_piece, s_piece))


def solution(mesh):
    return jax.shard_map(
        body,
        mesh=mesh,
        in_specs=(P(("hi", "lo"), None, None), P(None, "lo", None), P(None, "lo", None), P()),
        out_specs=P(("hi", "lo"), None, None),
        check_vma=False,
    )
```

```python
import functools

import jax
import jax.numpy as jnp
from jax import lax
from jax.experimental import pallas as pl
from jax.experimental.pallas import tpu as pltpu
from jax.sharding import PartitionSpec as P

MESH = pl.DeviceIdType.MESH
F32, BF16 = jnp.float32, jnp.bfloat16
N = 128
W = 1024
R = W // N
CH = 32


def split(v):
    top = v.astype(BF16)
    return top, (v - top.astype(F32)).astype(BF16)


def dot3(ah, al, bh, bl):
    d = functools.partial(jnp.dot, preferred_element_type=F32)
    return d(ah, bh) + (d(ah, bl) + d(al, bh))


def device_at(x, y, z, c):
    return z * 2 + x % 2, (x // 2) * 8 + y * 2 + c


def kernel(assign, stem, first, second, home, stage, turned, spread, f_all, s_all, pick, fh, fl, sh, sl, yh, yl,
           stage_sem, own_sem, self_sem, g_send, g_recv, x_send, x_recv, z_send, z_recv):
    hi, lo = lax.axis_index("hi"), lax.axis_index("lo")
    me = hi * 16 + lo
    x, y, z, c = (lo // 8) * 2 + hi % 2, (lo // 2) % 4, hi // 2, lo % 2
    xh, xl = x // 2, x % 2

    def load(q, slot):
        pltpu.make_async_copy(stem.at[:, pl.ds(q * CH, CH)], stage.at[slot], stage_sem.at[slot]).start()

    def relay(q, slot):
        pltpu.make_async_copy(stage.at[slot], stage.at[slot], stage_sem.at[slot]).wait()

        def one(t, _):
            block = stage[slot, :, pl.ds(pl.multiple_of(t * 8, 8), 8), :]
            rows = pl.ds(pl.multiple_of((q * CH + t * 8) * R, 8 * R), 8 * R)
            turned[rows, :] = pltpu.einshape("jmi->mji", block).reshape(8 * R, W)
            return 0

        lax.fori_loop(0, CH // 8, one, 0)

    own = [pltpu.make_async_copy(ref, pick.at[n], own_sem.at[n]) for n, ref in enumerate((first, second))]
    for copy in own:
        copy.start()
    for q in range(4):
        load(q, q)

    barrier = pltpu.get_barrier_semaphore()

    def greet(p):
        pl.semaphore_signal(barrier, inc=1, device_id=(p // 16, p % 16), device_id_type=MESH)

    def greet_far(t, _):
        greet((me + t + t // 15 + 1) % N)
        return 0

    lax.fori_loop(0, 120, greet_far, 0)
    for copy in own:
        copy.wait()
    for n, ref in enumerate((f_all, s_all)):
        ref[xh, y, c] = pick[n, assign[n]]
    for t in range(1, 8):
        greet((me + 16 * t) % N)
    for q in range(4):
        relay(q, q)
        load(q + 4, q)
    pl.semaphore_wait(barrier, N - 1)

    def remote(src, dst, send, recv, target):
        return pltpu.make_async_remote_copy(
            src_ref=src, dst_ref=dst, send_sem=send, recv_sem=recv, device_id=target, device_id_type=MESH
        )

    by_y = pl.ds(0, 16)
    by_z = pl.ds(pl.multiple_of(16 + 8 * z, 8), 8)
    by_x = pl.ds(pl.multiple_of(48 + 8 * xl, 8), 8)

    def pass_on(part, n, step, target):
        remote(part, part, g_send.at[n, step], g_recv.at[n, step], target).start()

    def gather_1(n, ref):
        pass_on(ref.at[xh, y, c, by_y], n, 0, device_at(3 - x, y, z, c))
        for t in range(1, 4):
            pass_on(ref.at[xh, y, c, by_x], n, 0, device_at(x, (y + t) % 4, z, c))
        for t in range(1, 8):
            pass_on(ref.at[xh, y, c, by_z], n, 0, device_at((x + 2 * (t // 4)) % 4, (y + t) % 4, z, c))

    def gather_2(n, ref):
        drain(96, recv=g_recv.at[n, 0])
        for t in range(1, 4):
            pass_on(ref.at[:, :, c, by_z], n, 1, device_at(x, y, (z + t) % 4, c))
            pass_on(ref.at[:, y, c, by_y], n, 1, device_at(x, (y + t) % 4, z, c))
            pass_on(ref.at[xh, :, c, by_x], n, 1, device_at((x + t) % 4, y, z, c))

    def gather_3(n, ref):
        drain(384, recv=g_recv.at[n, 1])
        pass_on(ref.at[:, :, c], n, 2, device_at(x, y, z, 1 - c))

    def offset(t):
        dc, u = t // 64, t % 64
        a, b, g = u % 4, (u // 4) % 4, u // 16
        target = device_at((x + a) % 4, (y + a + b) % 4, (z + a + b + g) % 4, (c + dc) % 2)
        return target, target[0] * 16 + target[1]

    my_rows = pl.ds(pl.multiple_of(me * R, R), R)

    def send_out(h):
        def one(t, _):
            target, p = offset(t)
            src = turned.at[pl.ds(pl.multiple_of((h * N + p) * R, R), R)]
            remote(src, spread.at[h, my_rows], x_send.at[h], x_recv.at[h], target).start()
            return 0

        lax.fori_loop(1, N, one, 0)
        own = pl.ds(pl.multiple_of((h * N + me) * R, R), R)
        pltpu.make_async_copy(turned.at[own], spread.at[h, my_rows], self_sem.at[h]).start()

    def send_home(h):
        own = pl.ds(pl.multiple_of((h * N + me) * R, R), R)

        def one(t, _):
            target, p = offset(t)
            src = spread.at[h, pl.ds(pl.multiple_of(p * R, R), R)]
            remote(src, home.at[own], z_send.at[h], z_recv.at[h], target).start()
            return 0

        lax.fori_loop(1, N, one, 0)
        pltpu.make_async_copy(spread.at[h, my_rows], home.at[own], self_sem.at[2 + h]).start()

    def rows_of(count):
        return spread.at[0, pl.ds(0, count)]

    def drain(count, send=None, recv=None):
        if send is not None:
            remote(rows_of(count), rows_of(count), send, send, (hi, lo)).wait_send()
        if recv is not None:
            remote(rows_of(count), rows_of(count), recv, recv, (hi, lo)).wait_recv()

    gather_1(0, f_all)
    gather_1(1, s_all)
    send_out(0)
    gather_2(0, f_all)
    gather_2(1, s_all)
    for q in range(4, 8):
        relay(q, q - 4)
    gather_3(0, f_all)
    send_out(1)

    drain(512, recv=g_recv.at[0, 2])

    def prepare_f(t, _):
        rows = pl.ds(pl.multiple_of(t * 64, 64), 64)
        fh[rows, :], fl[rows, :] = split(f_all[t // 8, (t // 2) % 4, t % 2])
        return 0

    lax.fori_loop(0, 16, prepare_f, 0)

    def prepare_s(t, _):
        p, cols = t // 8, pl.ds(pl.multiple_of((t % 8) * 128, 128), 128)
        block = jnp.concatenate([s_all[p // 4, p % 4, n, :, cols] for n in range(2)], axis=0)
        to = pl.ds(pl.multiple_of(p * 128, 128), 128)
        sh[cols, to], sl[cols, to] = split(block.T)
        return 0

    for h in range(2):
        pltpu.make_async_copy(turned.at[pl.ds(0, R)], spread.at[h, my_rows], self_sem.at[h]).wait()
        drain((N - 1) * R, recv=x_recv.at[h])

        def by_first(t, _):
            rows = pl.ds(pl.multiple_of(t * 256, 256), 256)
            ah, al = split(spread[h, rows, :])

            def tile(n, _):
                cols = pl.ds(pl.multiple_of(n * 256, 256), 256)
                yh[rows, cols], yl[rows, cols] = split(dot3(ah, al, fh[:, cols], fl[:, cols]))
                return 0

            return lax.fori_loop(0, 4, tile, 0)

        lax.fori_loop(0, 4, by_first, 0)
        if h == 0:
            gather_3(1, s_all)
            drain(512, recv=g_recv.at[1, 2])
            lax.fori_loop(0, 64, prepare_s, 0)

        def by_second(t, _):
            rows = pl.ds(pl.multiple_of((t // 4) * 256, 256), 256)
            cols = pl.ds(pl.multiple_of((t % 4) * 256, 256), 256)
            spread[h, rows, cols] = dot3(sh[rows, :], sl[rows, :], yh[:, cols], yl[:, cols])
            return 0

        lax.fori_loop(0, 16, by_second, 0)
        send_home(h)

    for n in range(2):
        drain(96, send=g_send.at[n, 0])
        drain(384, send=g_send.at[n, 1])
        drain(512, send=g_send.at[n, 2])
    for h in range(2):
        drain((N - 1) * R, send=x_send.at[h])
        drain((N - 1) * R, send=z_send.at[h])
        drain((N - 1) * R, recv=z_recv.at[h])
        pltpu.make_async_copy(turned.at[pl.ds(0, R)], spread.at[h, my_rows], self_sem.at[2 + h]).wait()


def exchange(stem, first, second, assign):
    dma = pltpu.SemaphoreType.DMA
    return pl.pallas_call(
        kernel,
        name="exchange",
        out_shape=pltpu.VMEM((stem.shape[1] * R, W), F32),
        in_specs=[pl.BlockSpec(memory_space=pltpu.SMEM)] + [pl.BlockSpec(memory_space=pl.ANY)] * 3,
        out_specs=pl.BlockSpec(memory_space=pltpu.VMEM),
        scratch_shapes=[
            pltpu.VMEM((4, R, CH, W), F32),
            pltpu.VMEM((2 * W, W), F32),
            pltpu.VMEM((2, W, W), F32),
            pltpu.VMEM((2, 4, 2, 64, W), F32),
            pltpu.VMEM((2, 4, 2, 64, W), F32),
            pltpu.VMEM((2, 8, 64, W), F32),
        ]
        + [pltpu.VMEM((W, W), BF16)] * 6
        + [dma((4,)), dma((2,)), dma((4,)), dma((2, 3)), dma((2, 3)), dma((2,)), dma((2,)), dma((2,)), dma((2,))],
        compiler_params=pltpu.CompilerParams(
            collective_id=0, has_side_effects=True, vmem_limit_bytes=54 << 20
        ),
    )(assign, stem, first, second)


def settle_kernel(home, out, turned, sem):
    m = home.shape[0] // R

    def piece(t, slot):
        return pltpu.make_async_copy(turned.at[slot], out.at[:, pl.ds(t * CH, CH)], sem.at[slot])

    def one(t, _):
        for u in range(CH // 8):
            rows = pl.ds(pl.multiple_of((t * CH + u * 8) * R, 8 * R), 8 * R)
            turned[t, :, pl.ds(u * 8, 8), :] = pltpu.einshape("mlk->lmk", home[rows, :].reshape(8, R, W))
        piece(t, t).start()
        return 0

    lax.fori_loop(0, m // CH, one, 0)
    for t in range(m // CH):
        piece(t, t).wait()


def settle(home):
    m = home.shape[0] // R
    return pl.pallas_call(
        settle_kernel,
        name="settle",
        out_shape=jax.ShapeDtypeStruct((R, m, W), F32),
        in_specs=[pl.BlockSpec(memory_space=pltpu.VMEM)],
        out_specs=pl.BlockSpec(memory_space=pl.ANY),
        scratch_shapes=[pltpu.VMEM((m // CH, R, CH, W), F32), pltpu.SemaphoreType.DMA((m // CH,))],
        compiler_params=pltpu.CompilerParams(vmem_limit_bytes=24 << 20),
    )(home)


def body(stem, first_branch, second_branch, assign):
    return settle(exchange(stem, first_branch, second_branch, assign))


def solution(mesh):
    return jax.shard_map(
        body,
        mesh=mesh,
        in_specs=(P(("hi", "lo"), None, None), P(None, "lo", None), P(None, "lo", None), P()),
        out_specs=P(("hi", "lo"), None, None),
        check_vma=False,
    )
```

```python
import functools

import jax
import jax.numpy as jnp
from jax import lax
from jax.experimental import pallas as pl
from jax.experimental.pallas import tpu as pltpu
from jax.sharding import PartitionSpec as P

MESH = pl.DeviceIdType.MESH
F32, BF16 = jnp.float32, jnp.bfloat16
N = 128
W = 1024
R = W // N
EARLY = 33
CH = 32


def div(a, b):
    return lax.div(a, jnp.int32(b))


def rem(a, b):
    return lax.rem(a, jnp.int32(b))


def split(v):
    top = v.astype(BF16)
    return top, (v - top.astype(F32)).astype(BF16)


def dot3(ah, al, bh, bl):
    d = functools.partial(jnp.dot, preferred_element_type=F32)
    return d(ah, bh) + (d(ah, bl) + d(al, bh))


def device_at(x, y, z, c):
    return z * 2 + rem(x, 2), div(x, 2) * 8 + y * 2 + c


def kernel(assign, stem, first, second, home, stage, turned, spread, f_all, s_all, pick, fh, fl, sh, sl, yh, yl,
           stage_sem, own_sem, self_sem, g_send, g_recv, x_send, x_recv, z_send, z_recv):
    hi, lo = lax.axis_index("hi"), lax.axis_index("lo")
    me = hi * 16 + lo
    x, y, z, c = (lo // 8) * 2 + hi % 2, (lo // 2) % 4, hi // 2, lo % 2
    xh, xl = x // 2, x % 2

    def load(q, slot):
        pltpu.make_async_copy(stem.at[:, pl.ds(q * CH, CH)], stage.at[slot], stage_sem.at[slot]).start()

    def relay(q, slot):
        pltpu.make_async_copy(stage.at[slot], stage.at[slot], stage_sem.at[slot]).wait()

        def one(t, _):
            block = stage[slot, :, pl.ds(pl.multiple_of(t * 8, 8), 8), :]
            rows = pl.ds(pl.multiple_of((q * CH + t * 8) * R, 8 * R), 8 * R)
            turned[rows, :] = pltpu.einshape("jmi->mji", block).reshape(8 * R, W)
            return 0

        lax.fori_loop(0, CH // 8, one, 0)

    own = [pltpu.make_async_copy(ref, pick.at[n], own_sem.at[n]) for n, ref in enumerate((first, second))]
    for copy in own:
        copy.start()
    for q in range(4):
        load(q, q)

    barrier = pltpu.get_barrier_semaphore()

    def greet(p):
        pl.semaphore_signal(barrier, inc=1, device_id=(div(p, 16), rem(p, 16)), device_id_type=MESH)

    def greet_far(t, _):
        other = rem(hi + t, 8)
        for k in range(1, 16):
            pl.semaphore_signal(barrier, inc=1, device_id=(other, rem(lo + k, 16)), device_id_type=MESH)
        return 0

    lax.fori_loop(0, 8, greet_far, 0)
    for copy in own:
        copy.wait()
    for n, ref in enumerate((f_all, s_all)):
        ref[xh, y, c] = pick[n, assign[n]]
    for t in range(1, 8):
        greet(rem(me + 16 * t, N))
    for q in range(4):
        relay(q, q)
        load(q + 4, q)
    pl.semaphore_wait(barrier, N - 1)

    def remote(src, dst, send, recv, target):
        return pltpu.make_async_remote_copy(
            src_ref=src, dst_ref=dst, send_sem=send, recv_sem=recv, device_id=target, device_id_type=MESH
        )

    by_y = pl.ds(0, 16)
    by_z = pl.ds(pl.multiple_of(16 + 8 * z, 8), 8)
    by_x = pl.ds(pl.multiple_of(48 + 8 * xl, 8), 8)

    def pass_on(part, n, step, target):
        remote(part, part, g_send.at[n, step], g_recv.at[n, step], target).start()

    def gather_1(n, ref):
        pass_on(ref.at[xh, y, c, by_y], n, 0, device_at(3 - x, y, z, c))
        for t in range(1, 4):
            pass_on(ref.at[xh, y, c, by_x], n, 0, device_at(x, (y + t) % 4, z, c))
        for t in range(1, 8):
            pass_on(ref.at[xh, y, c, by_z], n, 0, device_at((x + 2 * (t // 4)) % 4, (y + t) % 4, z, c))

    def gather_2(n, ref):
        drain(96, recv=g_recv.at[n, 0])
        for t in range(1, 4):
            pass_on(ref.at[:, :, c, by_z], n, 1, device_at(x, y, (z + t) % 4, c))
            pass_on(ref.at[:, y, c, by_y], n, 1, device_at(x, (y + t) % 4, z, c))
            pass_on(ref.at[xh, :, c, by_x], n, 1, device_at((x + t) % 4, y, z, c))

    def gather_3(n, ref):
        drain(384, recv=g_recv.at[n, 1])
        pass_on(ref.at[:, :, c], n, 2, device_at(x, y, z, 1 - c))

    def offset(t):
        dc, u = div(t, 64), rem(t, 64)
        a, b, g = rem(u, 4), rem(div(u, 4), 4), div(u, 16)
        target = device_at(rem(x + a, 4), rem(y + a + b, 4), rem(z + a + b + g, 4), rem(c + dc, 2))
        return target, target[0] * 16 + target[1]

    my_rows = pl.ds(pl.multiple_of(me * R, R), R)

    def send_out(h, begin, end):
        def one(t, _):
            target, p = offset(t)
            src = turned.at[pl.ds(pl.multiple_of((h * N + p) * R, R), R)]
            remote(src, spread.at[h, my_rows], x_send.at[h], x_recv.at[h], target).start()
            return 0

        lax.fori_loop(begin, end, one, 0)
        if end < N:
            return
        own = pl.ds(pl.multiple_of((h * N + me) * R, R), R)
        pltpu.make_async_copy(turned.at[own], spread.at[h, my_rows], self_sem.at[h]).start()

    def send_home(h):
        own = pl.ds(pl.multiple_of((h * N + me) * R, R), R)

        def one(t, _):
            target, p = offset(t)
            src = spread.at[h, pl.ds(pl.multiple_of(p * R, R), R)]
            remote(src, home.at[own], z_send.at[h], z_recv.at[h], target).start()
            return 0

        lax.fori_loop(1, N, one, 0)
        pltpu.make_async_copy(spread.at[h, my_rows], home.at[own], self_sem.at[2 + h]).start()

    def rows_of(count):
        return spread.at[0, pl.ds(0, count)]

    def drain(count, send=None, recv=None):
        if send is not None:
            remote(rows_of(count), rows_of(count), send, send, (hi, lo)).wait_send()
        if recv is not None:
            remote(rows_of(count), rows_of(count), recv, recv, (hi, lo)).wait_recv()

    gather_1(0, f_all)
    gather_1(1, s_all)
    send_out(0, 1, N)
    gather_2(0, f_all)
    gather_2(1, s_all)
    for q in range(4, 8):
        relay(q, q - 4)
    gather_3(0, f_all)
    send_out(1, 1, EARLY)
    gather_3(1, s_all)
    send_out(1, EARLY, N)

    drain(512, recv=g_recv.at[0, 2])

    def prepare_f(t, _):
        rows = pl.ds(pl.multiple_of(t * 64, 64), 64)
        fh[rows, :], fl[rows, :] = split(f_all[t // 8, (t // 2) % 4, t % 2])
        return 0

    lax.fori_loop(0, 16, prepare_f, 0)

    def prepare_s(t, _):
        p, cols = t // 8, pl.ds(pl.multiple_of((t % 8) * 128, 128), 128)
        block = jnp.concatenate([s_all[p // 4, p % 4, n, :, cols] for n in range(2)], axis=0)
        to = pl.ds(pl.multiple_of(p * 128, 128), 128)
        sh[cols, to], sl[cols, to] = split(block.T)
        return 0

    for h in range(2):
        pltpu.make_async_copy(turned.at[pl.ds(0, R)], spread.at[h, my_rows], self_sem.at[h]).wait()
        drain((N - 1) * R, recv=x_recv.at[h])

        def by_first(t, _):
            rows = pl.ds(pl.multiple_of(t * 256, 256), 256)
            ah, al = split(spread[h, rows, :])

            def tile(n, _):
                cols = pl.ds(pl.multiple_of(n * 256, 256), 256)
                yh[rows, cols], yl[rows, cols] = split(dot3(ah, al, fh[:, cols], fl[:, cols]))
                return 0

            return lax.fori_loop(0, 4, tile, 0)

        lax.fori_loop(0, 4, by_first, 0)
        if h == 0:
            drain(512, recv=g_recv.at[1, 2])
            lax.fori_loop(0, 64, prepare_s, 0)

        def by_second(t, _):
            rows = pl.ds(pl.multiple_of((t // 4) * 256, 256), 256)
            cols = pl.ds(pl.multiple_of((t % 4) * 256, 256), 256)
            spread[h, rows, cols] = dot3(sh[rows, :], sl[rows, :], yh[:, cols], yl[:, cols])
            return 0

        lax.fori_loop(0, 16, by_second, 0)
        send_home(h)

    for n in range(2):
        drain(96, send=g_send.at[n, 0])
        drain(384, send=g_send.at[n, 1])
        drain(512, send=g_send.at[n, 2])
    for h in range(2):
        drain((N - 1) * R, send=x_send.at[h])
        drain((N - 1) * R, send=z_send.at[h])
        drain((N - 1) * R, recv=z_recv.at[h])
        pltpu.make_async_copy(turned.at[pl.ds(0, R)], spread.at[h, my_rows], self_sem.at[2 + h]).wait()


def exchange(stem, first, second, assign):
    dma = pltpu.SemaphoreType.DMA
    return pl.pallas_call(
        kernel,
        name="exchange",
        out_shape=pltpu.VMEM((stem.shape[1] * R, W), F32),
        in_specs=[pl.BlockSpec(memory_space=pltpu.SMEM)] + [pl.BlockSpec(memory_space=pl.ANY)] * 3,
        out_specs=pl.BlockSpec(memory_space=pltpu.VMEM),
        scratch_shapes=[
            pltpu.VMEM((4, R, CH, W), F32),
            pltpu.VMEM((2 * W, W), F32),
            pltpu.VMEM((2, W, W), F32),
            pltpu.VMEM((2, 4, 2, 64, W), F32),
            pltpu.VMEM((2, 4, 2, 64, W), F32),
            pltpu.VMEM((2, 8, 64, W), F32),
        ]
        + [pltpu.VMEM((W, W), BF16)] * 6
        + [dma((4,)), dma((2,)), dma((4,)), dma((2, 3)), dma((2, 3)), dma((2,)), dma((2,)), dma((2,)), dma((2,))],
        compiler_params=pltpu.CompilerParams(
            collective_id=0, has_side_effects=True, vmem_limit_bytes=54 << 20
        ),
    )(assign, stem, first, second)


def settle_kernel(home, out, turned, sem):
    m = home.shape[0] // R

    def piece(t, slot):
        return pltpu.make_async_copy(turned.at[slot], out.at[:, pl.ds(t * CH, CH)], sem.at[slot])

    def one(t, _):
        for u in range(CH // 8):
            rows = pl.ds(pl.multiple_of((t * CH + u * 8) * R, 8 * R), 8 * R)
            turned[t, :, pl.ds(u * 8, 8), :] = pltpu.einshape("mlk->lmk", home[rows, :].reshape(8, R, W))
        piece(t, t).start()
        return 0

    lax.fori_loop(0, m // CH, one, 0)
    for t in range(m // CH):
        piece(t, t).wait()


def settle(home):
    m = home.shape[0] // R
    return pl.pallas_call(
        settle_kernel,
        name="settle",
        out_shape=jax.ShapeDtypeStruct((R, m, W), F32),
        in_specs=[pl.BlockSpec(memory_space=pltpu.VMEM)],
        out_specs=pl.BlockSpec(memory_space=pl.ANY),
        scratch_shapes=[pltpu.VMEM((m // CH, R, CH, W), F32), pltpu.SemaphoreType.DMA((m // CH,))],
        compiler_params=pltpu.CompilerParams(vmem_limit_bytes=24 << 20),
    )(home)


def body(stem, first_branch, second_branch, assign):
    return settle(exchange(stem, first_branch, second_branch, assign))


def solution(mesh):
    return jax.shard_map(
        body,
        mesh=mesh,
        in_specs=(P(("hi", "lo"), None, None), P(None, "lo", None), P(None, "lo", None), P()),
        out_specs=P(("hi", "lo"), None, None),
        check_vma=False,
    )
```

```python
import functools

import jax
import jax.numpy as jnp
from jax import lax
from jax.experimental import pallas as pl
from jax.experimental.pallas import tpu as pltpu
from jax.sharding import PartitionSpec as P

MESH = pl.DeviceIdType.MESH
F32, BF16 = jnp.float32, jnp.bfloat16
N = 128
W = 1024
R = W // N
FIRST = 64
EARLY = 33
CH = 32


def div(a, b):
    return lax.div(a, jnp.int32(b))


def rem(a, b):
    return lax.rem(a, jnp.int32(b))


def split(v):
    top = v.astype(BF16)
    return top, (v - top.astype(F32)).astype(BF16)


def dot3(ah, al, bh, bl):
    d = functools.partial(jnp.dot, preferred_element_type=F32)
    return d(ah, bh) + (d(ah, bl) + d(al, bh))


def device_at(x, y, z, c):
    return z * 2 + rem(x, 2), div(x, 2) * 8 + y * 2 + c


def kernel(assign, stem, first, second, home, stage, turned, spread, f_all, s_all, pick, fh, fl, sh, sl, yh, yl,
           stage_sem, own_sem, self_sem, g_send, g_recv, x_send, x_recv, z_send, z_recv):
    hi, lo = lax.axis_index("hi"), lax.axis_index("lo")
    me = hi * 16 + lo
    x, y, z, c = (lo // 8) * 2 + hi % 2, (lo // 2) % 4, hi // 2, lo % 2
    xh, xl = x // 2, x % 2

    def load(q, slot):
        pltpu.make_async_copy(stem.at[:, pl.ds(q * CH, CH)], stage.at[slot], stage_sem.at[slot]).start()

    def relay(q, slot):
        pltpu.make_async_copy(stage.at[slot], stage.at[slot], stage_sem.at[slot]).wait()

        def one(t, _):
            block = stage[slot, :, pl.ds(pl.multiple_of(t * 8, 8), 8), :]
            rows = pl.ds(pl.multiple_of((q * CH + t * 8) * R, 8 * R), 8 * R)
            turned[rows, :] = pltpu.einshape("jmi->mji", block).reshape(8 * R, W)
            return 0

        lax.fori_loop(0, CH // 8, one, 0)

    own = [pltpu.make_async_copy(ref, pick.at[n], own_sem.at[n]) for n, ref in enumerate((first, second))]
    for copy in own:
        copy.start()
    for q in range(4):
        load(q, q)

    barrier = pltpu.get_barrier_semaphore()

    def greet(t, _):
        other = rem(hi + t, 8)
        for k in range(1, 16):
            pl.semaphore_signal(barrier, inc=1, device_id=(other, rem(lo + k, 16)), device_id_type=MESH)

        @pl.when(t > 0)
        def _():
            pl.semaphore_signal(barrier, inc=1, device_id=(other, lo), device_id_type=MESH)

        return 0

    lax.fori_loop(0, 8, greet, 0)
    for copy in own:
        copy.wait()
    for n, ref in enumerate((f_all, s_all)):
        ref[xh, y, c] = pick[n, assign[n]]
    for q in range(4):
        relay(q, q)
        load(q + 4, q)
    pl.semaphore_wait(barrier, N - 1)

    def remote(src, dst, send, recv, target):
        return pltpu.make_async_remote_copy(
            src_ref=src, dst_ref=dst, send_sem=send, recv_sem=recv, device_id=target, device_id_type=MESH
        )

    up = [rem(v + 1, 4) for v in (x, y, z)]
    down = [rem(v + 3, 4) for v in (x, y, z)]
    chip = xh * 4 + y

    def y_rows(half):
        return pl.ds(8 * half, 8)

    def z_rows(layer):
        return pl.ds(pl.multiple_of(16 + 8 * layer, 8), 8)

    def x_rows(column):
        return pl.ds(pl.multiple_of(48 + 8 * rem(column, 2), 8), 8)

    def pass_on(part, n, step, target):
        remote(part, part, g_send.at[n, step], g_recv.at[n, step], target).start()

    def gather_1(n, ref):
        for half in range(2):
            pass_on(ref.at[xh, y, c, y_rows(half)], n, 0, device_at(3 - x, y, z, c))
        for t in range(1, 4):
            pass_on(ref.at[xh, y, c, x_rows(x)], n, 0, device_at(x, rem(y + t, 4), z, c))
        for t in range(1, 8):
            target = device_at(rem(x + 2 * (t // 4), 4), rem(y + t, 4), z, c)
            pass_on(ref.at[xh, y, c, z_rows(z)], n, 0, target)

    def gather_2(n, ref):
        drain(96, recv=g_recv.at[n, 0])
        for side in (up, down):
            def along_z(t, _):
                other = rem(chip + t, 8)
                pass_on(ref.at[div(other, 4), rem(other, 4), c, z_rows(z)], n, 1, device_at(x, y, side[2], c))
                return 0

            lax.fori_loop(1, 8, along_z, 0)
            for e in range(2):
                for half in range(2):
                    pass_on(ref.at[e, y, c, y_rows(half)], n, 1, device_at(x, side[1], z, c))
            for t in range(1, 4):
                pass_on(ref.at[xh, rem(y + t, 4), c, x_rows(x)], n, 1, device_at(side[0], y, z, c))

            @pl.when(div(side[0], 2) != xh)
            def _():
                pass_on(ref.at[xh, y, c, x_rows(x)], n, 1, device_at(side[0], y, z, c))

    def gather_3(n, ref):
        drain(232, recv=g_recv.at[n, 1])

        def along_z(t, _):
            other = rem(chip + t, 8)
            e = div(other, 4)
            back, forth = rem(z + 3 + 2 * e, 4), rem(z + 1 + 2 * e, 4)
            pass_on(ref.at[e, rem(other, 4), c, z_rows(back)], n, 2, device_at(x, y, forth, c))
            return 0

        lax.fori_loop(1, 8, along_z, 0)
        for e, back, forth in ((0, down, up), (1, up, down)):
            for half in range(2):
                pass_on(ref.at[e, back[1], c, y_rows(half)], n, 2, device_at(x, forth[1], z, c))
                part = ref.at[div(back[0], 2), 2 * e + half, c, x_rows(back[0])]
                pass_on(part, n, 2, device_at(forth[0], y, z, c))

    def gather_4(n, ref):
        drain(120, recv=g_recv.at[n, 2])
        pass_on(ref.at[:, :, c], n, 3, device_at(x, y, z, 1 - c))

    def offset(t):
        dc, u = div(t, 64), rem(t, 64)
        a, b, g = rem(u, 4), rem(div(u, 4), 4), div(u, 16)
        target = device_at(rem(x + a, 4), rem(y + a + b, 4), rem(z + a + b + g, 4), rem(c + dc, 2))
        return target, target[0] * 16 + target[1]

    my_rows = pl.ds(pl.multiple_of(me * R, R), R)

    def send_out(h, begin, end):
        def one(t, _):
            target, p = offset(t)
            src = turned.at[pl.ds(pl.multiple_of((h * N + p) * R, R), R)]
            remote(src, spread.at[h, my_rows], x_send.at[h], x_recv.at[h], target).start()
            return 0

        lax.fori_loop(begin, end, one, 0)
        if end < N:
            return
        own = pl.ds(pl.multiple_of((h * N + me) * R, R), R)
        pltpu.make_async_copy(turned.at[own], spread.at[h, my_rows], self_sem.at[h]).start()

    def send_home(h):
        own = pl.ds(pl.multiple_of((h * N + me) * R, R), R)

        def one(t, _):
            target, p = offset(t)
            src = spread.at[h, pl.ds(pl.multiple_of(p * R, R), R)]
            remote(src, home.at[own], z_send.at[h], z_recv.at[h], target).start()
            return 0

        lax.fori_loop(1, N, one, 0)
        pltpu.make_async_copy(spread.at[h, my_rows], home.at[own], self_sem.at[2 + h]).start()

    def rows_of(count):
        return spread.at[0, pl.ds(0, count)]

    def drain(count, send=None, recv=None):
        if send is not None:
            remote(rows_of(count), rows_of(count), send, send, (hi, lo)).wait_send()
        if recv is not None:
            remote(rows_of(count), rows_of(count), recv, recv, (hi, lo)).wait_recv()

    gather_1(0, f_all)
    gather_1(1, s_all)
    send_out(0, 1, FIRST)
    gather_2(0, f_all)
    gather_2(1, s_all)
    send_out(0, FIRST, N)
    for q in range(4, 8):
        relay(q, q - 4)
    gather_3(0, f_all)
    gather_3(1, s_all)
    send_out(1, 1, EARLY)
    gather_4(0, f_all)
    gather_4(1, s_all)
    send_out(1, EARLY, N)

    drain(512, recv=g_recv.at[0, 3])

    def prepare_f(t, _):
        rows = pl.ds(pl.multiple_of(t * 64, 64), 64)
        fh[rows, :], fl[rows, :] = split(f_all[t // 8, (t // 2) % 4, t % 2])
        return 0

    lax.fori_loop(0, 16, prepare_f, 0)

    def prepare_s(t, _):
        p, cols = t // 8, pl.ds(pl.multiple_of((t % 8) * 128, 128), 128)
        block = jnp.concatenate([s_all[p // 4, p % 4, n, :, cols] for n in range(2)], axis=0)
        to = pl.ds(pl.multiple_of(p * 128, 128), 128)
        sh[cols, to], sl[cols, to] = split(block.T)
        return 0

    for h in range(2):
        pltpu.make_async_copy(turned.at[pl.ds(0, R)], spread.at[h, my_rows], self_sem.at[h]).wait()
        drain((N - 1) * R, recv=x_recv.at[h])

        def by_first(t, _):
            rows = pl.ds(pl.multiple_of(t * 256, 256), 256)
            ah, al = split(spread[h, rows, :])

            def tile(n, _):
                cols = pl.ds(pl.multiple_of(n * 256, 256), 256)
                yh[rows, cols], yl[rows, cols] = split(dot3(ah, al, fh[:, cols], fl[:, cols]))
                return 0

            return lax.fori_loop(0, 4, tile, 0)

        lax.fori_loop(0, 4, by_first, 0)
        if h == 0:
            drain(512, recv=g_recv.at[1, 3])
            lax.fori_loop(0, 64, prepare_s, 0)

        def by_second(t, _):
            rows = pl.ds(pl.multiple_of((t // 4) * 256, 256), 256)
            cols = pl.ds(pl.multiple_of((t % 4) * 256, 256), 256)
            spread[h, rows, cols] = dot3(sh[rows, :], sl[rows, :], yh[:, cols], yl[:, cols])
            return 0

        lax.fori_loop(0, 16, by_second, 0)
        send_home(h)

    for n in range(2):
        drain(96, send=g_send.at[n, 0])
        drain(232, send=g_send.at[n, 1])
        drain(120, send=g_send.at[n, 2])
        drain(512, send=g_send.at[n, 3])
    for h in range(2):
        drain((N - 1) * R, send=x_send.at[h])
        drain((N - 1) * R, send=z_send.at[h])
        drain((N - 1) * R, recv=z_recv.at[h])
        pltpu.make_async_copy(turned.at[pl.ds(0, R)], spread.at[h, my_rows], self_sem.at[2 + h]).wait()


def exchange(stem, first, second, assign):
    dma = pltpu.SemaphoreType.DMA
    return pl.pallas_call(
        kernel,
        name="exchange",
        out_shape=pltpu.VMEM((stem.shape[1] * R, W), F32),
        in_specs=[pl.BlockSpec(memory_space=pltpu.SMEM)] + [pl.BlockSpec(memory_space=pl.ANY)] * 3,
        out_specs=pl.BlockSpec(memory_space=pltpu.VMEM),
        scratch_shapes=[
            pltpu.VMEM((4, R, CH, W), F32),
            pltpu.VMEM((2 * W, W), F32),
            pltpu.VMEM((2, W, W), F32),
            pltpu.VMEM((2, 4, 2, 64, W), F32),
            pltpu.VMEM((2, 4, 2, 64, W), F32),
            pltpu.VMEM((2, 8, 64, W), F32),
        ]
        + [pltpu.VMEM((W, W), BF16)] * 6
        + [dma((4,)), dma((2,)), dma((4,)), dma((2, 4)), dma((2, 4)), dma((2,)), dma((2,)), dma((2,)), dma((2,))],
        compiler_params=pltpu.CompilerParams(
            collective_id=0, has_side_effects=True, vmem_limit_bytes=54 << 20
        ),
    )(assign, stem, first, second)


def settle_kernel(home, out, turned, sem):
    m = home.shape[0] // R

    def piece(t, slot):
        return pltpu.make_async_copy(turned.at[slot], out.at[:, pl.ds(t * CH, CH)], sem.at[slot])

    def one(t, _):
        for u in range(CH // 8):
            rows = pl.ds(pl.multiple_of((t * CH + u * 8) * R, 8 * R), 8 * R)
            turned[t, :, pl.ds(u * 8, 8), :] = pltpu.einshape("mlk->lmk", home[rows, :].reshape(8, R, W))
        piece(t, t).start()
        return 0

    lax.fori_loop(0, m // CH, one, 0)
    for t in range(m // CH):
        piece(t, t).wait()


def settle(home):
    m = home.shape[0] // R
    return pl.pallas_call(
        settle_kernel,
        name="settle",
        out_shape=jax.ShapeDtypeStruct((R, m, W), F32),
        in_specs=[pl.BlockSpec(memory_space=pltpu.VMEM)],
        out_specs=pl.BlockSpec(memory_space=pl.ANY),
        scratch_shapes=[pltpu.VMEM((m // CH, R, CH, W), F32), pltpu.SemaphoreType.DMA((m // CH,))],
        compiler_params=pltpu.CompilerParams(vmem_limit_bytes=24 << 20),
    )(home)


def body(stem, first_branch, second_branch, assign):
    return settle(exchange(stem, first_branch, second_branch, assign))


def solution(mesh):
    return jax.shard_map(
        body,
        mesh=mesh,
        in_specs=(P(("hi", "lo"), None, None), P(None, "lo", None), P(None, "lo", None), P()),
        out_specs=P(("hi", "lo"), None, None),
        check_vma=False,
    )
```
